1024 devices in a mesh: src: 8 (over x, y_hi), space: 128 (over z, y_lo, core).
Axes of the slice: x: 4, y: 8 (y_hi: 2, y_lo: 4; y = y_hi * 4 + y_lo), z: 16, core: 2. Of those that a mesh axis runs over, the one named last changes fastest.
Arguments:
- vectors: bfloat16 [3, 2, 147456, 128], P(None, None, 'space', 'src'), may hold values from -0.015625 to 0.015625
- lambdas: float32 [3, 128], replicated, may hold values from 0.01 to 0.2
- sources: bfloat16 [2, 147456, 1024], P(None, 'space', 'src'), may hold values from -6 to 6
Outputs:
- propagated: bfloat16 [2, 147456, 1024], P(None, 'space', 'src')
The draws below stay inside these ranges and needn't reach their ends.
All inputs are finite; a program needn't handle non-finite values.
Results may differ from the reference program's by a relative error of at most 0.0049.
Values may be sent and summed in bfloat16 or wider, within the bound.
A program may use at most 32 MiB of HBM per device.

```python
import math
import jax
import jax.numpy as jnp

GROUP_MODES = 128
GROUPS = 3
ROWS = 147456
COLS = 1024


def level_of(key, extent, pieces, smallest, high):
    def one(position, parts):
        draws = jax.random.uniform(jax.random.fold_in(jax.random.fold_in(key, 6), position), (parts,), jnp.float32, smallest / len(pieces), high / len(pieces))
        return jnp.repeat(jnp.exp(draws), extent[position] // parts).reshape((-1,) + (1,) * (len(extent) - position - 1))

    level = one(*pieces[0])
    for cut in pieces[1:]:
        level = level * one(*cut)
    return level


def bell_draw(key, shape, scale, reach, split=(), dtype=jnp.bfloat16):
    drawn = jax.random.normal(key, shape, jnp.float32) * scale
    if len(split) > 0:
        drawn = level_of(key, shape, split, -0.22, 0.18) * drawn
    return jnp.clip(drawn, min=-reach, max=reach).astype(dtype)


def setup_inputs(seed: int = 0) -> dict:
    splits = jax.random.split(jax.random.key(seed), 4)
    return {
        "vectors": bell_draw(splits[0], (GROUPS, 2, ROWS, GROUP_MODES), ROWS ** -0.5, 0.015625, ((2, 128), (3, 8))),
        "lambdas": jnp.clip(jnp.exp(jax.random.uniform(splits[1], (GROUPS, GROUP_MODES), jnp.float32, math.log(0.01), math.log(0.2))), 0.01, 0.2),
        "sources": bell_draw(splits[2], (2, ROWS, COLS), 1.0, 6.0, ((1, 128), (2, 8))),
    }


def reference(vectors, lambdas, sources):
    src_re = sources[0]
    src_im = sources[1]
    out_re = jnp.zeros((ROWS, COLS), jnp.float32)
    out_im = jnp.zeros((ROWS, COLS), jnp.float32)
    for number in range(GROUPS):
        vec_re = vectors[number, 0]
        vec_im = vectors[number, 1]
        coef_re = jnp.dot(vec_re.T, src_re, preferred_element_type=jnp.float32) + jnp.dot(vec_im.T, src_im, preferred_element_type=jnp.float32)
        coef_im = jnp.dot(vec_re.T, src_im, preferred_element_type=jnp.float32) - jnp.dot(vec_im.T, src_re, preferred_element_type=jnp.float32)
        factor = (1.0 / lambdas[number])[:, None]
        scaled_re = (coef_re * factor).astype(jnp.bfloat16)
        scaled_im = (coef_im * factor).astype(jnp.bfloat16)
        out_re = out_re + jnp.dot(vec_re, scaled_re, preferred_element_type=jnp.float32) - jnp.dot(vec_im, scaled_im, preferred_element_type=jnp.float32)
        out_im = out_im + jnp.dot(vec_re, scaled_im, preferred_element_type=jnp.float32) + jnp.dot(vec_im, scaled_re, preferred_element_type=jnp.float32)
    return jnp.stack([out_re, out_im]).astype(jnp.bfloat16)
```

```python
import jax
import jax.numpy as jnp
from jax import lax
from jax.experimental import pallas as pl
from jax.experimental.pallas import tpu as pltpu
from jax.sharding import PartitionSpec as P

G = 3
XS = 4
YS = 8
YL = 4
ZS = 16

YU, YD, PR, PI, L0, L1, R0, R1, O0, O1, QL0, QL1, QR0, QR1, QO0, QO1 = range(16)
EVENTS = 16


def kernel(
    vec, lam, srcs, out,
    vt, vrow, rhs1, rhs2, relay, acc,
    coef, crecv, zsrc, zrecv, ysrc, yrecv, sg,
    local_sem, ag_send, ag_recv,
    c_send, c_recv, z_send, z_recv, y_send, y_recv, s_send, s_recv, d_send, d_recv,
):
    me = lax.axis_index("src")
    space = lax.axis_index("space")
    x, h = me // 2, me % 2
    core, yl, z = space % 2, (space // 2) % YL, space // (2 * YL)
    y = h * YL + yl

    def at(x_, y_, z_, core_):
        return (x_ * 2 + y_ // YL, (z_ * YL + y_ % YL) * 2 + core_)

    right = at((x + 1) % XS, y, z, core)
    left = at((x + XS - 1) % XS, y, z, core)
    up = at(x, (y + 2) % YS, z, core)
    down = at(x, (y + YS - 2) % YS, z, core)
    sibling = at(x, y, z, 1 - core)
    z_peer = lambda k: at(x, y, (z + k) % ZS, core)
    y_peer = lambda k: at(x, h * YL + (yl + k) % YL, z, core)

    own = me
    mate = x * 2 + (1 - h)
    mate_up = x * 2 + (1 - ((y + 2) % YS) // YL)
    mate_down = x * 2 + (1 - ((y + YS - 2) % YS) // YL)
    xl, xr, xo = (x + XS - 1) % XS, (x + 1) % XS, (x + 2) % XS
    bl, br, bo = xl * 2 + h, xr * 2 + h, xo * 2 + h
    ql, qr, qo = xl * 2 + (1 - h), xr * 2 + (1 - h), xo * 2 + (1 - h)

    barrier = pltpu.get_barrier_semaphore()
    for peer in (right, left, up, down, sibling):
        pl.semaphore_signal(barrier, inc=1, device_id=peer, device_id_type=pl.DeviceIdType.MESH)
    for k in range(1, YL):
        pl.semaphore_signal(barrier, inc=1, device_id=y_peer(k), device_id_type=pl.DeviceIdType.MESH)

    @pl.loop(1, ZS)
    def _(k):
        pl.semaphore_signal(barrier, inc=1, device_id=z_peer(k), device_id_type=pl.DeviceIdType.MESH)

    loads = [
        pltpu.make_async_copy(vec, vt.at[:, :, own], local_sem.at[0]),
        pltpu.make_async_copy(srcs.at[0], rhs1.at[:, pl.ds(0, 128)], local_sem.at[1]),
        pltpu.make_async_copy(srcs.at[1], rhs1.at[:, pl.ds(128, 128)], local_sem.at[2]),
        pltpu.make_async_copy(srcs.at[1], rhs2.at[:, pl.ds(0, 128)], local_sem.at[3]),
    ]
    for load in loads:
        load.start()
    pl.semaphore_wait(barrier, 5 + (YL - 1) + (ZS - 1))

    sent = []

    def send(src, dst, g, event, device):
        copy = pltpu.make_async_remote_copy(
            src_ref=src, dst_ref=dst, send_sem=ag_send.at[g, event], recv_sem=ag_recv.at[g, event],
            device_id=device, device_id_type=pl.DeviceIdType.MESH,
        )
        copy.start()
        sent.append(copy)

    def arrived(region, g, event):
        pltpu.make_async_remote_copy(
            src_ref=region, dst_ref=region, send_sem=ag_send.at[g, event], recv_sem=ag_recv.at[g, event],
            device_id=right, device_id_type=pl.DeviceIdType.MESH,
        ).wait_recv()

    def start_own(g):
        send(vec.at[g, 0], relay.at[g, 0], g, YU, up)
        send(vec.at[g, 1], relay.at[g, 1], g, YD, down)
        send(vec.at[g, 0], vt.at[g, 0, own], g, L0, right)
        send(vec.at[g, 1], vt.at[g, 1, own], g, R1, left)
        send(vec.at[g, 1], vt.at[g, 1, own], g, L1, right)
        send(vec.at[g, 0], vt.at[g, 0, own], g, R0, left)

    def relay_y(g):
        arrived(relay.at[g, 0], g, YU)
        send(relay.at[g, 0], vt.at[g, 0, mate_up], g, PR, up)
        arrived(relay.at[g, 1], g, YD)
        send(relay.at[g, 1], vt.at[g, 1, mate_down], g, PI, down)

    def relay_x(g):
        arrived(vt.at[g, 0, bl], g, L0)
        send(vt.at[g, 0, bl], vt.at[g, 0, bl], g, O0, right)
        arrived(vt.at[g, 1, br], g, R1)
        send(vt.at[g, 1, br], vt.at[g, 1, br], g, O1, left)

    def start_mate(g):
        arrived(vt.at[g, 0, mate], g, PR)
        send(vt.at[g, 0, mate], vt.at[g, 0, mate], g, QL0, right)
        arrived(vt.at[g, 1, mate], g, PI)
        send(vt.at[g, 1, mate], vt.at[g, 1, mate], g, QR1, left)
        send(vt.at[g, 1, mate], vt.at[g, 1, mate], g, QL1, right)
        send(vt.at[g, 0, mate], vt.at[g, 0, mate], g, QR0, left)

    def relay_mate(g):
        arrived(vt.at[g, 0, ql], g, QL0)
        send(vt.at[g, 0, ql], vt.at[g, 0, ql], g, QO0, right)
        arrived(vt.at[g, 1, qr], g, QR1)
        send(vt.at[g, 1, qr], vt.at[g, 1, qr], g, QO1, left)

    def finish_gather(g):
        for event, c, block in (
            (L1, 1, bl), (R0, 0, br), (O0, 0, bo), (O1, 1, bo),
            (QL1, 1, ql), (QR0, 0, qr), (QO0, 0, qo), (QO1, 1, qo),
        ):
            arrived(vt.at[g, c, block], g, event)

    c_copies = [
        pltpu.make_async_remote_copy(
            src_ref=coef.at[g, 1 - core], dst_ref=crecv.at[g], send_sem=c_send.at[g], recv_sem=c_recv.at[g],
            device_id=sibling, device_id_type=pl.DeviceIdType.MESH,
        )
        for g in range(G)
    ]
    d_copies = [
        pltpu.make_async_remote_copy(
            src_ref=sg.at[g, core], dst_ref=sg.at[g, core], send_sem=d_send.at[g], recv_sem=d_recv.at[g],
            device_id=sibling, device_id_type=pl.DeviceIdType.MESH,
        )
        for g in range(G)
    ]

    def project(g):
        part = jnp.dot(vt[g, 0].reshape(128, -1), rhs1[...], preferred_element_type=jnp.float32)
        part = part + jnp.dot(vt[g, 1].reshape(128, -1), rhs2[...], preferred_element_type=jnp.float32)
        for half in range(2):
            for c in range(2):
                coef[g, half, c] = part[64 * half : 64 * half + 64, 128 * c : 128 * c + 128]
        c_copies[g].start()

    def z_copy(g, k):
        return pltpu.make_async_remote_copy(
            src_ref=zsrc.at[g, (z + k) % ZS], dst_ref=zrecv.at[g, ZS - 1 - k],
            send_sem=z_send.at[g], recv_sem=z_recv.at[g],
            device_id=z_peer(k), device_id_type=pl.DeviceIdType.MESH,
        )

    def scatter_z(g):
        c_copies[g].wait_recv()
        zsrc[g] = (coef[g, core] + crecv[g]).reshape(ZS, 8, 128)

        @pl.loop(1, ZS)
        def _(k):
            z_copy(g, k).start()

    def all_of(ref, send_sem, recv_sem):
        return pltpu.make_async_remote_copy(
            src_ref=ref, dst_ref=ref, send_sem=send_sem, recv_sem=recv_sem,
            device_id=right, device_id_type=pl.DeviceIdType.MESH,
        )

    def y_copy(g, k):
        return pltpu.make_async_remote_copy(
            src_ref=ysrc.at[g], dst_ref=yrecv.at[g, YL - 1 - k],
            send_sem=y_send.at[g], recv_sem=y_recv.at[g],
            device_id=y_peer(k), device_id_type=pl.DeviceIdType.MESH,
        )

    def exchange_y(g):
        all_of(zrecv.at[g], z_send.at[g], z_recv.at[g]).wait_recv()
        total = zsrc[g, z]
        for k in range(ZS - 1):
            total = total + zrecv[g, k]
        ysrc[g] = total
        for k in range(1, YL):
            y_copy(g, k).start()

    row = lax.broadcasted_iota(jnp.int32, (8, 128), 0)

    def s_copy(g, k):
        return pltpu.make_async_remote_copy(
            src_ref=sg.at[g, core, z], dst_ref=sg.at[g, core, z],
            send_sem=s_send.at[g], recv_sem=s_recv.at[g],
            device_id=z_peer(k), device_id_type=pl.DeviceIdType.MESH,
        )

    def scale(g):
        first = 64 * core + 8 * (z % 8)
        values = jnp.full((8, 128), lam[g, first], jnp.float32)
        for i in range(1, 8):
            values = jnp.where(row == i, lam[g, first + i], values)
        inverse = 1.0 / values
        all_of(yrecv.at[g], y_send.at[g], y_recv.at[g]).wait_recv()
        total = ysrc[g] + yrecv[g, 0] + yrecv[g, 1] + yrecv[g, 2]
        sg[g, core, z] = (total * inverse).astype(jnp.bfloat16).astype(jnp.float32)

        @pl.loop(1, ZS)
        def _(k):
            s_copy(g, k).start()

    def share(g):
        all_of(sg.at[g, core, pl.ds(0, ZS - 1)], s_send.at[g], s_recv.at[g]).wait_recv()
        d_copies[g].start()

    def transposed(g):
        for c in range(2):
            vrow[g, :, 128 * c : 128 * c + 128] = vt[g, c].reshape(128, -1).T

    def expand(g):
        all_of(sg.at[g, 1 - core], d_send.at[g], d_recv.at[g]).wait_recv()
        re = jnp.concatenate([sg[g, 0, 0:8].reshape(64, 128), sg[g, 1, 0:8].reshape(64, 128)], axis=0)
        im = jnp.concatenate([sg[g, 0, 8:16].reshape(64, 128), sg[g, 1, 8:16].reshape(64, 128)], axis=0)
        re = re.astype(jnp.bfloat16)
        im = im.astype(jnp.bfloat16)
        factor = jnp.concatenate(
            [jnp.concatenate([re, im], axis=1), jnp.concatenate([-im, re], axis=1)], axis=0
        )
        product = jnp.dot(vrow[g], factor, preferred_element_type=jnp.float32)
        if g == 0:
            acc[...] = product
        elif g < G - 1:
            acc[...] += product
        else:
            total = (acc[...] + product).astype(jnp.bfloat16)
            out[0] = total[:, :128]
            out[1] = total[:, 128:]

    for g in range(G):
        start_own(g)
    for load in loads:
        load.wait()
    rhs2[:, 128:256] = -rhs1[:, 0:128]

    relay_y(0)
    relay_x(0)
    relay_y(1)
    relay_x(1)
    start_mate(0)
    relay_y(2)
    relay_x(2)
    start_mate(1)
    relay_mate(0)
    start_mate(2)
    finish_gather(0)
    project(0)
    relay_mate(1)
    scatter_z(0)
    finish_gather(1)
    project(1)
    relay_mate(2)
    scatter_z(1)
    finish_gather(2)
    project(2)
    scatter_z(2)
    for g in range(G):
        transposed(g)
    exchange_y(0)
    exchange_y(1)
    scale(0)
    exchange_y(2)
    scale(1)
    scale(2)
    share(0)
    expand(0)
    share(1)
    expand(1)
    share(2)
    expand(2)

    for copy in sent:
        copy.wait_send()
    for g in range(G):
        c_copies[g].wait_send()
        d_copies[g].wait_send()
        all_of(zrecv.at[g], z_send.at[g], z_recv.at[g]).wait_send()
        all_of(yrecv.at[g], y_send.at[g], y_recv.at[g]).wait_send()
        all_of(sg.at[g, core, pl.ds(0, ZS - 1)], s_send.at[g], s_recv.at[g]).wait_send()


def on_device(vectors, lambdas, sources):
    rows = sources.shape[1]
    cols = sources.shape[2]
    vec = jnp.transpose(vectors, (0, 1, 3, 2))
    f32, bf16 = jnp.float32, jnp.bfloat16
    dma = pltpu.SemaphoreType.DMA
    return pl.pallas_call(
        kernel,
        out_shape=jax.ShapeDtypeStruct((2, rows, cols), bf16),
        in_specs=[
            pl.BlockSpec(memory_space=pl.ANY),
            pl.BlockSpec(memory_space=pltpu.SMEM),
            pl.BlockSpec(memory_space=pl.ANY),
        ],
        out_specs=pl.BlockSpec(memory_space=pltpu.VMEM),
        scratch_shapes=[
            pltpu.VMEM((G, 2, 8, 16, rows), bf16),
            pltpu.VMEM((G, rows, 256), bf16),
            pltpu.VMEM((rows, 256), bf16),
            pltpu.VMEM((rows, 256), bf16),
            pltpu.VMEM((G, 2, 16, rows), bf16),
            pltpu.VMEM((rows, 256), f32),
            pltpu.VMEM((G, 2, 2, 64, 128), f32),
            pltpu.VMEM((G, 2, 64, 128), f32),
            pltpu.VMEM((G, ZS, 8, 128), f32),
            pltpu.VMEM((G, ZS - 1, 8, 128), f32),
            pltpu.VMEM((G, 8, 128), f32),
            pltpu.VMEM((G, YL - 1, 8, 128), f32),
            pltpu.VMEM((G, 2, ZS, 8, 128), f32),
            dma((4,)),
            dma((G, EVENTS)),
            dma((G, EVENTS)),
            dma((G,)), dma((G,)), dma((G,)), dma((G,)), dma((G,)), dma((G,)),
            dma((G,)), dma((G,)), dma((G,)), dma((G,)),
        ],
        compiler_params=pltpu.CompilerParams(collective_id=0, has_side_effects=True),
    )(vec, lambdas, sources)


def solution(mesh):
    placed = (P(None, None, "space", "src"), P(), P(None, "space", "src"))
    return jax.shard_map(
        on_device, mesh=mesh, in_specs=placed, out_specs=P(None, "space", "src"), check_vma=False
    )
```

```python
import jax
import jax.numpy as jnp
from jax import lax
from jax.experimental import pallas as pl
from jax.experimental.pallas import tpu as pltpu
from jax.sharding import PartitionSpec as P

G = 3
XS = 4
YS = 8
YL = 4
ZS = 16

PR, PI, L0, L1, R0, R1, O0, O1, QL0, QL1, QR0, QR1, QO0, QO1 = range(14)
EVENTS = 14


def kernel(
    vec, lam, srcs, out,
    vt, vrow, rhs1, rhs2, acc,
    coef, crecv, zsrc, zrecv, ysrc, yrecv, sg,
    ready, local_sem, ag_send, ag_recv,
    c_send, c_recv, z_send, z_recv, y_send, y_recv, s_send, s_recv, d_send, d_recv,
):
    me = lax.axis_index("src")
    space = lax.axis_index("space")
    x, h = me // 2, me % 2
    core, yl, z = space % 2, (space // 2) % YL, space // (2 * YL)
    y = h * YL + yl

    def at(x_, y_, z_, core_):
        return (x_ * 2 + y_ // YL, (z_ * YL + y_ % YL) * 2 + core_)

    right = at((x + 1) % XS, y, z, core)
    left = at((x + XS - 1) % XS, y, z, core)
    across = at(x, (y + YL) % YS, z, core)
    sibling = at(x, y, z, 1 - core)
    z_peer = lambda k: at(x, y, (z + k) % ZS, core)
    y_peer = lambda k: at(x, h * YL + (yl + k) % YL, z, core)

    own = me
    mate = x * 2 + (1 - h)
    xl, xr, xo = (x + XS - 1) % XS, (x + 1) % XS, (x + 2) % XS
    bl, br, bo = xl * 2 + h, xr * 2 + h, xo * 2 + h
    ql, qr, qo = xl * 2 + (1 - h), xr * 2 + (1 - h), xo * 2 + (1 - h)

    def signal(semaphore, device):
        pl.semaphore_signal(semaphore, inc=1, device_id=device, device_id_type=pl.DeviceIdType.MESH)

    def greet(semaphore, step):
        pl.when(z >= step)(lambda: signal(semaphore, at(x, y, z - step, core)))
        pl.when(z + step < ZS)(lambda: signal(semaphore, at(x, y, z + step, core)))

    def greeters(step):
        return jnp.where(z >= step, 1, 0) + jnp.where(z + step < ZS, 1, 0)

    barrier = pltpu.get_barrier_semaphore()
    for peer in (right, left, across, sibling):
        signal(barrier, peer)
    for k in range(1, YL):
        signal(barrier, y_peer(k))
    greet(barrier, 1)

    def meet(round_):
        pl.semaphore_wait(ready.at[round_], greeters(1 << round_))
        if round_ < 3:
            greet(ready.at[round_ + 1], 2 << round_)

    loads = [
        pltpu.make_async_copy(vec, vt.at[:, :, own], local_sem.at[0]),
        pltpu.make_async_copy(srcs.at[0], rhs1.at[:, pl.ds(0, 128)], local_sem.at[1]),
        pltpu.make_async_copy(srcs.at[1], rhs1.at[:, pl.ds(128, 128)], local_sem.at[2]),
        pltpu.make_async_copy(srcs.at[1], rhs2.at[:, pl.ds(0, 128)], local_sem.at[3]),
    ]
    for load in loads:
        load.start()
    pl.semaphore_wait(barrier, 4 + (YL - 1) + greeters(1))
    greet(ready.at[0], 1)

    sent = []

    def send(src, dst, g, event, device):
        copy = pltpu.make_async_remote_copy(
            src_ref=src, dst_ref=dst, send_sem=ag_send.at[g, event], recv_sem=ag_recv.at[g, event],
            device_id=device, device_id_type=pl.DeviceIdType.MESH,
        )
        copy.start()
        sent.append(copy)

    def arrived(region, g, event):
        pltpu.make_async_remote_copy(
            src_ref=region, dst_ref=region, send_sem=ag_send.at[g, event], recv_sem=ag_recv.at[g, event],
            device_id=right, device_id_type=pl.DeviceIdType.MESH,
        ).wait_recv()

    def start_own(g):
        send(vec.at[g, 0], vt.at[g, 0, own], g, PR, across)
        send(vec.at[g, 1], vt.at[g, 1, own], g, PI, across)
        send(vec.at[g, 0], vt.at[g, 0, own], g, L0, right)
        send(vec.at[g, 1], vt.at[g, 1, own], g, R1, left)
        send(vec.at[g, 1], vt.at[g, 1, own], g, L1, right)
        send(vec.at[g, 0], vt.at[g, 0, own], g, R0, left)

    def relay_x(g):
        arrived(vt.at[g, 0, bl], g, L0)
        send(vt.at[g, 0, bl], vt.at[g, 0, bl], g, O0, right)
        arrived(vt.at[g, 1, br], g, R1)
        send(vt.at[g, 1, br], vt.at[g, 1, br], g, O1, left)

    def start_mate(g):
        arrived(vt.at[g, 0, mate], g, PR)
        send(vt.at[g, 0, mate], vt.at[g, 0, mate], g, QL0, right)
        arrived(vt.at[g, 1, mate], g, PI)
        send(vt.at[g, 1, mate], vt.at[g, 1, mate], g, QR1, left)
        send(vt.at[g, 1, mate], vt.at[g, 1, mate], g, QL1, right)
        send(vt.at[g, 0, mate], vt.at[g, 0, mate], g, QR0, left)

    def relay_mate(g):
        arrived(vt.at[g, 0, ql], g, QL0)
        send(vt.at[g, 0, ql], vt.at[g, 0, ql], g, QO0, right)
        arrived(vt.at[g, 1, qr], g, QR1)
        send(vt.at[g, 1, qr], vt.at[g, 1, qr], g, QO1, left)

    def finish_gather(g):
        for event, c, block in (
            (L1, 1, bl), (R0, 0, br), (O0, 0, bo), (O1, 1, bo),
            (QL1, 1, ql), (QR0, 0, qr), (QO0, 0, qo), (QO1, 1, qo),
        ):
            arrived(vt.at[g, c, block], g, event)

    c_copies = [
        pltpu.make_async_remote_copy(
            src_ref=coef.at[g, 1 - core], dst_ref=crecv.at[g], send_sem=c_send.at[g], recv_sem=c_recv.at[g],
            device_id=sibling, device_id_type=pl.DeviceIdType.MESH,
        )
        for g in range(G)
    ]
    d_copies = [
        pltpu.make_async_remote_copy(
            src_ref=sg.at[g, core], dst_ref=sg.at[g, core], send_sem=d_send.at[g], recv_sem=d_recv.at[g],
            device_id=sibling, device_id_type=pl.DeviceIdType.MESH,
        )
        for g in range(G)
    ]

    def project(g):
        part = jnp.dot(vt[g, 0].reshape(128, -1), rhs1[...], preferred_element_type=jnp.float32)
        part = part + jnp.dot(vt[g, 1].reshape(128, -1), rhs2[...], preferred_element_type=jnp.float32)
        for half in range(2):
            for c in range(2):
                coef[g, half, c] = part[64 * half : 64 * half + 64, 128 * c : 128 * c + 128]
        c_copies[g].start()

    def far_first(j):
        return ZS // 2 + ((j + 1) // 2) * (2 * ((j + 1) % 2) - 1)

    def z_copy(g, k):
        return pltpu.make_async_remote_copy(
            src_ref=zsrc.at[g, (z + k) % ZS], dst_ref=zrecv.at[g, ZS - 1 - k],
            send_sem=z_send.at[g], recv_sem=z_recv.at[g],
            device_id=z_peer(k), device_id_type=pl.DeviceIdType.MESH,
        )

    def scatter_z(g):
        c_copies[g].wait_recv()
        zsrc[g] = (coef[g, core] + crecv[g]).reshape(ZS, 8, 128)

        @pl.loop(0, ZS - 1)
        def _(j):
            z_copy(g, far_first(j)).start()

    def all_of(ref, send_sem, recv_sem):
        return pltpu.make_async_remote_copy(
            src_ref=ref, dst_ref=ref, send_sem=send_sem, recv_sem=recv_sem,
            device_id=right, device_id_type=pl.DeviceIdType.MESH,
        )

    def y_copy(g, k):
        return pltpu.make_async_remote_copy(
            src_ref=ysrc.at[g], dst_ref=yrecv.at[g, YL - 1 - k],
            send_sem=y_send.at[g], recv_sem=y_recv.at[g],
            device_id=y_peer(k), device_id_type=pl.DeviceIdType.MESH,
        )

    def exchange_y(g):
        all_of(zrecv.at[g], z_send.at[g], z_recv.at[g]).wait_recv()
        total = zsrc[g, z]
        for k in range(ZS - 1):
            total = total + zrecv[g, k]
        ysrc[g] = total
        for k in range(1, YL):
            y_copy(g, k).start()

    row = lax.broadcasted_iota(jnp.int32, (8, 128), 0)

    def s_copy(g, k):
        return pltpu.make_async_remote_copy(
            src_ref=sg.at[g, core, z], dst_ref=sg.at[g, core, z],
            send_sem=s_send.at[g], recv_sem=s_recv.at[g],
            device_id=z_peer(k), device_id_type=pl.DeviceIdType.MESH,
        )

    def scale(g):
        first = 64 * core + 8 * (z % 8)
        values = jnp.full((8, 128), lam[g, first], jnp.float32)
        for i in range(1, 8):
            values = jnp.where(row == i, lam[g, first + i], values)
        inverse = 1.0 / values
        all_of(yrecv.at[g], y_send.at[g], y_recv.at[g]).wait_recv()
        total = ysrc[g] + yrecv[g, 0] + yrecv[g, 1] + yrecv[g, 2]
        sg[g, core, z] = (total * inverse).astype(jnp.bfloat16)

        @pl.loop(0, ZS - 1)
        def _(j):
            s_copy(g, far_first(j)).start()

    def share(g):
        all_of(sg.at[g, core, pl.ds(0, ZS - 1)], s_send.at[g], s_recv.at[g]).wait_recv()
        d_copies[g].start()

    def transposed(g):
        for c in range(2):
            vrow[g, :, 128 * c : 128 * c + 128] = vt[g, c].reshape(128, -1).T

    def expand(g):
        all_of(sg.at[g, 1 - core], d_send.at[g], d_recv.at[g]).wait_recv()
        tiles = lambda part: [
            sg[g, half, part].astype(jnp.float32).reshape(64, 128) for half in range(2)
        ]
        re = jnp.concatenate(tiles(slice(0, 8)), axis=0).astype(jnp.bfloat16)
        im = jnp.concatenate(tiles(slice(8, 16)), axis=0).astype(jnp.bfloat16)
        factor = jnp.concatenate(
            [jnp.concatenate([re, im], axis=1), jnp.concatenate([-im, re], axis=1)], axis=0
        )
        product = jnp.dot(vrow[g], factor, preferred_element_type=jnp.float32)
        if g == 0:
            acc[...] = product
        elif g < G - 1:
            acc[...] += product
        else:
            total = acc[...] + product
            out[0] = total[:, :128]
            out[1] = total[:, 128:]

    for g in range(G):
        start_own(g)
    for load in loads:
        load.wait()
    rhs2[:, 128:256] = -rhs1[:, 0:128]

    meet(0)
    relay_x(0)
    relay_x(1)
    meet(1)
    relay_x(2)
    start_mate(0)
    meet(2)
    start_mate(1)
    relay_mate(0)
    start_mate(2)
    relay_mate(1)
    finish_gather(0)
    project(0)
    meet(3)
    scatter_z(0)
    relay_mate(2)
    finish_gather(1)
    project(1)
    scatter_z(1)
    finish_gather(2)
    project(2)
    scatter_z(2)
    for g in range(G):
        transposed(g)
    exchange_y(0)
    exchange_y(1)
    scale(0)
    exchange_y(2)
    scale(1)
    scale(2)
    share(0)
    expand(0)
    share(1)
    expand(1)
    share(2)
    expand(2)

    for copy in sent:
        copy.wait_send()
    for g in range(G):
        c_copies[g].wait_send()
        d_copies[g].wait_send()
        all_of(zrecv.at[g], z_send.at[g], z_recv.at[g]).wait_send()
        all_of(yrecv.at[g], y_send.at[g], y_recv.at[g]).wait_send()
        all_of(sg.at[g, core, pl.ds(0, ZS - 1)], s_send.at[g], s_recv.at[g]).wait_send()


def on_device(vectors, lambdas, sources):
    rows = sources.shape[1]
    cols = sources.shape[2]
    vec = jnp.transpose(vectors, (0, 1, 3, 2))
    f32, bf16 = jnp.float32, jnp.bfloat16
    dma = pltpu.SemaphoreType.DMA
    total = pl.pallas_call(
        kernel,
        out_shape=jax.ShapeDtypeStruct((2, rows, cols), f32),
        in_specs=[
            pl.BlockSpec(memory_space=pl.ANY),
            pl.BlockSpec(memory_space=pltpu.SMEM),
            pl.BlockSpec(memory_space=pl.ANY),
        ],
        out_specs=pl.BlockSpec(memory_space=pltpu.VMEM),
        scratch_shapes=[
            pltpu.VMEM((G, 2, 8, 16, rows), bf16),
            pltpu.VMEM((G, rows, 256), bf16),
            pltpu.VMEM((rows, 256), bf16),
            pltpu.VMEM((rows, 256), bf16),
            pltpu.VMEM((rows, 256), f32),
            pltpu.VMEM((G, 2, 2, 64, 128), f32),
            pltpu.VMEM((G, 2, 64, 128), f32),
            pltpu.VMEM((G, ZS, 8, 128), f32),
            pltpu.VMEM((G, ZS - 1, 8, 128), f32),
            pltpu.VMEM((G, 8, 128), f32),
            pltpu.VMEM((G, YL - 1, 8, 128), f32),
            pltpu.VMEM((G, 2, ZS, 8, 128), bf16),
            pltpu.SemaphoreType.REGULAR((4,)),
            dma((4,)),
            dma((G, EVENTS)),
            dma((G, EVENTS)),
            dma((G,)), dma((G,)), dma((G,)), dma((G,)), dma((G,)), dma((G,)),
            dma((G,)), dma((G,)), dma((G,)), dma((G,)),
        ],
        compiler_params=pltpu.CompilerParams(collective_id=0, has_side_effects=True),
    )(vec, lambdas, sources)
    return total.astype(bf16)


def solution(mesh):
    placed = (P(None, None, "space", "src"), P(), P(None, "space", "src"))
    return jax.shard_map(
        on_device, mesh=mesh, in_specs=placed, out_specs=P(None, "space", "src"), check_vma=False
    )
```

```python
import jax
import jax.numpy as jnp
from jax import lax
from jax.experimental import pallas as pl
from jax.experimental.pallas import tpu as pltpu
from jax.sharding import PartitionSpec as P

G = 3
XS = 4
YS = 8
YL = 4
ZS = 16

PR, PI, L0, L1, R0, R1, O0, O1, QL0, QL1, QR0, QR1, QO0, QO1 = range(14)
EVENTS = 14


def kernel(
    vec, lam, srcs, out,
    vt, vrow, rhs1, rhs2, acc,
    coef, crecv, zsrc, zrecv, ysrc, yrecv, sg,
    ready, local_sem, ag_send, ag_recv,
    c_send, c_recv, z_send, z_recv, y_send, y_recv, s_send, s_recv, d_send, d_recv,
):
    me = lax.axis_index("src")
    space = lax.axis_index("space")
    x, h = me // 2, me % 2
    core, yl, z = space % 2, (space // 2) % YL, space // (2 * YL)
    y = h * YL + yl

    def at(x_, y_, z_, core_):
        return (x_ * 2 + y_ // YL, (z_ * YL + y_ % YL) * 2 + core_)

    right = at((x + 1) % XS, y, z, core)
    left = at((x + XS - 1) % XS, y, z, core)
    across = at(x, (y + YL) % YS, z, core)
    sibling = at(x, y, z, 1 - core)
    z_peer = lambda k: at(x, y, (z + k) % ZS, core)
    y_peer = lambda k: at(x, h * YL + (yl + k) % YL, z, core)

    own = me
    mate = x * 2 + (1 - h)
    xl, xr, xo = (x + XS - 1) % XS, (x + 1) % XS, (x + 2) % XS
    bl, br, bo = xl * 2 + h, xr * 2 + h, xo * 2 + h
    ql, qr, qo = xl * 2 + (1 - h), xr * 2 + (1 - h), xo * 2 + (1 - h)

    def signal(semaphore, device):
        pl.semaphore_signal(semaphore, inc=1, device_id=device, device_id_type=pl.DeviceIdType.MESH)

    def greet(semaphore, step):
        pl.when(z >= step)(lambda: signal(semaphore, at(x, y, z - step, core)))
        pl.when(z + step < ZS)(lambda: signal(semaphore, at(x, y, z + step, core)))

    def greeters(step):
        return jnp.where(z >= step, 1, 0) + jnp.where(z + step < ZS, 1, 0)

    barrier = pltpu.get_barrier_semaphore()
    for peer in (right, left, across, sibling):
        signal(barrier, peer)
    for k in range(1, YL):
        signal(barrier, y_peer(k))
    greet(barrier, 1)

    def meet(round_):
        pl.semaphore_wait(ready.at[round_], greeters(1 << round_))
        if round_ < 3:
            greet(ready.at[round_ + 1], 2 << round_)

    loads = [
        pltpu.make_async_copy(vec, vt.at[:, :, own], local_sem.at[0]),
        pltpu.make_async_copy(srcs.at[0], rhs1.at[:, pl.ds(0, 128)], local_sem.at[1]),
        pltpu.make_async_copy(srcs.at[1], rhs1.at[:, pl.ds(128, 128)], local_sem.at[2]),
        pltpu.make_async_copy(srcs.at[1], rhs2.at[:, pl.ds(0, 128)], local_sem.at[3]),
    ]
    for load in loads:
        load.start()
    pl.semaphore_wait(barrier, 4 + (YL - 1) + greeters(1))
    greet(ready.at[0], 1)

    sent = []

    def send(src, dst, g, event, device):
        copy = pltpu.make_async_remote_copy(
            src_ref=src, dst_ref=dst, send_sem=ag_send.at[g, event], recv_sem=ag_recv.at[g, event],
            device_id=device, device_id_type=pl.DeviceIdType.MESH,
        )
        copy.start()
        sent.append(copy)

    def arrived(region, g, event):
        pltpu.make_async_remote_copy(
            src_ref=region, dst_ref=region, send_sem=ag_send.at[g, event], recv_sem=ag_recv.at[g, event],
            device_id=right, device_id_type=pl.DeviceIdType.MESH,
        ).wait_recv()

    def start_own(g):
        send(vec.at[g, 0], vt.at[g, 0, own], g, PR, across)
        send(vec.at[g, 1], vt.at[g, 1, own], g, PI, across)
        send(vec.at[g, 0], vt.at[g, 0, own], g, L0, right)
        send(vec.at[g, 1], vt.at[g, 1, own], g, R1, left)
        send(vec.at[g, 1], vt.at[g, 1, own], g, L1, right)
        send(vec.at[g, 0], vt.at[g, 0, own], g, R0, left)

    def relay_x(g):
        arrived(vt.at[g, 0, bl], g, L0)
        send(vt.at[g, 0, bl], vt.at[g, 0, bl], g, O0, right)
        arrived(vt.at[g, 1, br], g, R1)
        send(vt.at[g, 1, br], vt.at[g, 1, br], g, O1, left)

    def start_mate(g):
        arrived(vt.at[g, 0, mate], g, PR)
        send(vt.at[g, 0, mate], vt.at[g, 0, mate], g, QL0, right)
        arrived(vt.at[g, 1, mate], g, PI)
        send(vt.at[g, 1, mate], vt.at[g, 1, mate], g, QR1, left)
        send(vt.at[g, 1, mate], vt.at[g, 1, mate], g, QL1, right)
        send(vt.at[g, 0, mate], vt.at[g, 0, mate], g, QR0, left)

    def relay_mate(g):
        arrived(vt.at[g, 0, ql], g, QL0)
        send(vt.at[g, 0, ql], vt.at[g, 0, ql], g, QO0, right)
        arrived(vt.at[g, 1, qr], g, QR1)
        send(vt.at[g, 1, qr], vt.at[g, 1, qr], g, QO1, left)

    def opposite_across(g):
        for event, c, mate_event in ((O0, 0, QO0), (O1, 1, QO1)):
            arrived(vt.at[g, c, bo], g, event)
            send(vt.at[g, c, bo], vt.at[g, c, bo], g, mate_event, across)

    def finish_gather(g):
        for event, c, block in (
            (L1, 1, bl), (R0, 0, br), (O0, 0, bo), (O1, 1, bo), (QL0, 0, ql), (QR1, 1, qr),
            (QL1, 1, ql), (QR0, 0, qr), (QO0, 0, qo), (QO1, 1, qo),
        ):
            if event in ((QL0, QR1) if g < G - 1 else (O0, O1)):
                continue
            arrived(vt.at[g, c, block], g, event)

    c_copies = [
        pltpu.make_async_remote_copy(
            src_ref=coef.at[g, 1 - core], dst_ref=crecv.at[g], send_sem=c_send.at[g], recv_sem=c_recv.at[g],
            device_id=sibling, device_id_type=pl.DeviceIdType.MESH,
        )
        for g in range(G)
    ]
    def project(g):
        part = jnp.dot(vt[g, 0].reshape(128, -1), rhs1[...], preferred_element_type=jnp.float32)
        part = part + jnp.dot(vt[g, 1].reshape(128, -1), rhs2[...], preferred_element_type=jnp.float32)
        for half in range(2):
            for c in range(2):
                coef[g, half, c] = part[64 * half : 64 * half + 64, 128 * c : 128 * c + 128]
        c_copies[g].start()

    def far_first(j):
        return ZS // 2 + ((j + 1) // 2) * (2 * ((j + 1) % 2) - 1)

    def z_copy(g, k):
        return pltpu.make_async_remote_copy(
            src_ref=zsrc.at[g, (z + k) % ZS], dst_ref=zrecv.at[g, ZS - 1 - k],
            send_sem=z_send.at[g], recv_sem=z_recv.at[g],
            device_id=z_peer(k), device_id_type=pl.DeviceIdType.MESH,
        )

    def scatter_z(g):
        c_copies[g].wait_recv()
        zsrc[g] = (coef[g, core] + crecv[g]).reshape(ZS, 8, 128)

        for j in range(ZS - 1):
            z_copy(g, far_first(j)).start()

    def all_of(ref, send_sem, recv_sem):
        return pltpu.make_async_remote_copy(
            src_ref=ref, dst_ref=ref, send_sem=send_sem, recv_sem=recv_sem,
            device_id=right, device_id_type=pl.DeviceIdType.MESH,
        )

    def y_copy(g, k):
        return pltpu.make_async_remote_copy(
            src_ref=ysrc.at[g], dst_ref=yrecv.at[g, YL - 1 - k],
            send_sem=y_send.at[g], recv_sem=y_recv.at[g],
            device_id=y_peer(k), device_id_type=pl.DeviceIdType.MESH,
        )

    def exchange_y(g):
        all_of(zrecv.at[g], z_send.at[g], z_recv.at[g]).wait_recv()
        total = zsrc[g, z]
        for k in range(ZS - 1):
            total = total + zrecv[g, k]
        ysrc[g] = total
        for k in range(1, YL):
            y_copy(g, k).start()

    row = lax.broadcasted_iota(jnp.int32, (8, 128), 0)

    def s_copy(g, k):
        return pltpu.make_async_remote_copy(
            src_ref=sg.at[g, core, z], dst_ref=sg.at[g, core, z],
            send_sem=s_send.at[g], recv_sem=s_recv.at[g],
            device_id=at(x, y, k, core), device_id_type=pl.DeviceIdType.MESH,
        )

    def d_copy(g, k):
        return pltpu.make_async_remote_copy(
            src_ref=sg.at[g, core, z], dst_ref=sg.at[g, core, z],
            send_sem=d_send.at[g], recv_sem=d_recv.at[g],
            device_id=at(x, y, k, 1 - core), device_id_type=pl.DeviceIdType.MESH,
        )

    def scale(g):
        first = 64 * core + 8 * (z % 8)
        values = jnp.full((8, 128), lam[g, first], jnp.float32)
        for i in range(1, 8):
            values = jnp.where(row == i, lam[g, first + i], values)
        inverse = 1.0 / values
        all_of(yrecv.at[g], y_send.at[g], y_recv.at[g]).wait_recv()
        total = ysrc[g] + yrecv[g, 0] + yrecv[g, 1] + yrecv[g, 2]
        sg[g, core, z] = (total * inverse).astype(jnp.bfloat16)

        for target in range(ZS):
            d_copy(g, target).start()

            @pl.when(z != target)
            def _(target=target):
                s_copy(g, target).start()

    def share(g):
        all_of(sg.at[g, core, pl.ds(0, ZS - 1)], s_send.at[g], s_recv.at[g]).wait_recv()

    def transposed(g):
        for c in range(2):
            vrow[g, :, 128 * c : 128 * c + 128] = vt[g, c].reshape(128, -1).T

    def expand(g):
        all_of(sg.at[g, 1 - core], d_send.at[g], d_recv.at[g]).wait_recv()
        tiles = lambda part: [
            sg[g, half, part].astype(jnp.float32).reshape(64, 128) for half in range(2)
        ]
        re = jnp.concatenate(tiles(slice(0, 8)), axis=0).astype(jnp.bfloat16)
        im = jnp.concatenate(tiles(slice(8, 16)), axis=0).astype(jnp.bfloat16)
        factor = jnp.concatenate(
            [jnp.concatenate([re, im], axis=1), jnp.concatenate([-im, re], axis=1)], axis=0
        )
        product = jnp.dot(vrow[g], factor, preferred_element_type=jnp.float32)
        if g == 0:
            acc[...] = product
        elif g < G - 1:
            acc[...] += product
        else:
            total = acc[...] + product
            out[0] = total[:, :128]
            out[1] = total[:, 128:]

    for g in range(G):
        start_own(g)
    for load in loads:
        load.wait()
    rhs2[:, 128:256] = -rhs1[:, 0:128]

    meet(0)
    relay_x(0)
    relay_x(1)
    meet(1)
    relay_x(2)
    start_mate(0)
    meet(2)
    opposite_across(2)
    start_mate(1)
    relay_mate(0)
    relay_mate(1)
    finish_gather(0)
    project(0)
    start_mate(2)
    meet(3)
    scatter_z(0)
    finish_gather(1)
    project(1)
    scatter_z(1)
    finish_gather(2)
    project(2)
    scatter_z(2)
    for g in range(G):
        transposed(g)
    exchange_y(0)
    exchange_y(1)
    scale(0)
    exchange_y(2)
    scale(1)
    scale(2)
    share(0)
    expand(0)
    share(1)
    expand(1)
    share(2)
    expand(2)

    for copy in sent:
        copy.wait_send()
    for g in range(G):
        c_copies[g].wait_send()
        all_of(sg.at[g, core], d_send.at[g], d_recv.at[g]).wait_send()
        all_of(zrecv.at[g], z_send.at[g], z_recv.at[g]).wait_send()
        all_of(yrecv.at[g], y_send.at[g], y_recv.at[g]).wait_send()
        all_of(sg.at[g, core, pl.ds(0, ZS - 1)], s_send.at[g], s_recv.at[g]).wait_send()


def on_device(vectors, lambdas, sources):
    rows = sources.shape[1]
    cols = sources.shape[2]
    vec = jnp.transpose(vectors, (0, 1, 3, 2))
    f32, bf16 = jnp.float32, jnp.bfloat16
    dma = pltpu.SemaphoreType.DMA
    total = pl.pallas_call(
        kernel,
        out_shape=jax.ShapeDtypeStruct((2, rows, cols), f32),
        in_specs=[
            pl.BlockSpec(memory_space=pl.ANY),
            pl.BlockSpec(memory_space=pltpu.SMEM),
            pl.BlockSpec(memory_space=pl.ANY),
        ],
        out_specs=pl.BlockSpec(memory_space=pltpu.VMEM),
        scratch_shapes=[
            pltpu.VMEM((G, 2, 8, 16, rows), bf16),
            pltpu.VMEM((G, rows, 256), bf16),
            pltpu.VMEM((rows, 256), bf16),
            pltpu.VMEM((rows, 256), bf16),
            pltpu.VMEM((rows, 256), f32),
            pltpu.VMEM((G, 2, 2, 64, 128), f32),
            pltpu.VMEM((G, 2, 64, 128), f32),
            pltpu.VMEM((G, ZS, 8, 128), f32),
            pltpu.VMEM((G, ZS - 1, 8, 128), f32),
            pltpu.VMEM((G, 8, 128), f32),
            pltpu.VMEM((G, YL - 1, 8, 128), f32),
            pltpu.VMEM((G, 2, ZS, 8, 128), bf16),
            pltpu.SemaphoreType.REGULAR((4,)),
            dma((4,)),
            dma((G, EVENTS)),
            dma((G, EVENTS)),
            dma((G,)), dma((G,)), dma((G,)), dma((G,)), dma((G,)), dma((G,)),
            dma((G,)), dma((G,)), dma((G,)), dma((G,)),
        ],
        compiler_params=pltpu.CompilerParams(collective_id=0, has_side_effects=True),
    )(vec, lambdas, sources)
    return total.astype(bf16)


def solution(mesh):
    placed = (P(None, None, "space", "src"), P(), P(None, "space", "src"))
    return jax.shard_map(
        on_device, mesh=mesh, in_specs=placed, out_specs=P(None, "space", "src"), check_vma=False
    )
```

```python
import jax
import jax.numpy as jnp
from jax import lax
from jax.experimental import pallas as pl
from jax.experimental.pallas import tpu as pltpu
from jax.sharding import PartitionSpec as P

G = 3
XS = 4
YS = 8
YL = 4
ZS = 16
DIRECT = (2,)

PR, PI, L0, L1, R0, R1, O0, O1, QL0, QL1, QR0, QR1, QO0, QO1 = range(14)
EVENTS = 14


def kernel(
    vec, lam, srcs, out,
    vt, vrow, rhs1, rhs2, acc,
    coef, crecv, zsrc, zrecv, ysrc, yrecv, sg,
    ready, local_sem, ag_send, ag_recv,
    c_send, c_recv, z_send, z_recv, y_send, y_recv, s_send, s_recv, d_send, d_recv,
):
    me = lax.axis_index("src")
    space = lax.axis_index("space")
    x, h = me // 2, me % 2
    core, yl, z = space % 2, (space // 2) % YL, space // (2 * YL)
    y = h * YL + yl

    def at(x_, y_, z_, core_):
        return (x_ * 2 + y_ // YL, (z_ * YL + y_ % YL) * 2 + core_)

    right = at((x + 1) % XS, y, z, core)
    left = at((x + XS - 1) % XS, y, z, core)
    across = at(x, (y + YL) % YS, z, core)
    sibling = at(x, y, z, 1 - core)
    z_peer = lambda k: at(x, y, (z + k) % ZS, core)
    y_peer = lambda k: at(x, h * YL + (yl + k) % YL, z, core)

    own = me
    mate = x * 2 + (1 - h)
    xl, xr, xo = (x + XS - 1) % XS, (x + 1) % XS, (x + 2) % XS
    bl, br, bo = xl * 2 + h, xr * 2 + h, xo * 2 + h
    ql, qr, qo = xl * 2 + (1 - h), xr * 2 + (1 - h), xo * 2 + (1 - h)

    def signal(semaphore, device):
        pl.semaphore_signal(semaphore, inc=1, device_id=device, device_id_type=pl.DeviceIdType.MESH)

    def greet(semaphore, step):
        pl.when(z >= step)(lambda: signal(semaphore, at(x, y, z - step, core)))
        pl.when(z + step < ZS)(lambda: signal(semaphore, at(x, y, z + step, core)))

    def greeters(step):
        return jnp.where(z >= step, 1, 0) + jnp.where(z + step < ZS, 1, 0)

    barrier = pltpu.get_barrier_semaphore()
    for peer in (right, left, across, sibling):
        signal(barrier, peer)
    for k in range(1, YL):
        signal(barrier, y_peer(k))
    greet(barrier, 1)

    def meet(round_):
        pl.semaphore_wait(ready.at[round_], greeters(1 << round_))
        if round_ < 3:
            greet(ready.at[round_ + 1], 2 << round_)

    loads = [
        pltpu.make_async_copy(vec, vt.at[:, :, own], local_sem.at[0]),
        pltpu.make_async_copy(srcs.at[0], rhs1.at[:, pl.ds(0, 128)], local_sem.at[1]),
        pltpu.make_async_copy(srcs.at[1], rhs1.at[:, pl.ds(128, 128)], local_sem.at[2]),
        pltpu.make_async_copy(srcs.at[1], rhs2.at[:, pl.ds(0, 128)], local_sem.at[3]),
    ]
    for load in loads:
        load.start()
    pl.semaphore_wait(barrier, 4 + (YL - 1) + greeters(1))
    greet(ready.at[0], 1)

    sent = []

    def send(src, dst, g, event, device):
        copy = pltpu.make_async_remote_copy(
            src_ref=src, dst_ref=dst, send_sem=ag_send.at[g, event], recv_sem=ag_recv.at[g, event],
            device_id=device, device_id_type=pl.DeviceIdType.MESH,
        )
        copy.start()
        sent.append(copy)

    def arrived(region, g, event):
        pltpu.make_async_remote_copy(
            src_ref=region, dst_ref=region, send_sem=ag_send.at[g, event], recv_sem=ag_recv.at[g, event],
            device_id=right, device_id_type=pl.DeviceIdType.MESH,
        ).wait_recv()

    def start_own(g):
        send(vec.at[g, 0], vt.at[g, 0, own], g, PR, across)
        send(vec.at[g, 1], vt.at[g, 1, own], g, PI, across)
        send(vec.at[g, 0], vt.at[g, 0, own], g, L0, right)
        send(vec.at[g, 1], vt.at[g, 1, own], g, R1, left)
        send(vec.at[g, 1], vt.at[g, 1, own], g, L1, right)
        send(vec.at[g, 0], vt.at[g, 0, own], g, R0, left)

    def relay_x(g):
        arrived(vt.at[g, 0, bl], g, L0)
        send(vt.at[g, 0, bl], vt.at[g, 0, bl], g, O0, right)
        arrived(vt.at[g, 1, br], g, R1)
        send(vt.at[g, 1, br], vt.at[g, 1, br], g, O1, left)

    def start_mate(g):
        arrived(vt.at[g, 0, mate], g, PR)
        send(vt.at[g, 0, mate], vt.at[g, 0, mate], g, QL0, right)
        arrived(vt.at[g, 1, mate], g, PI)
        send(vt.at[g, 1, mate], vt.at[g, 1, mate], g, QR1, left)
        send(vt.at[g, 1, mate], vt.at[g, 1, mate], g, QL1, right)
        send(vt.at[g, 0, mate], vt.at[g, 0, mate], g, QR0, left)

    def relay_mate(g):
        arrived(vt.at[g, 0, ql], g, QL0)
        send(vt.at[g, 0, ql], vt.at[g, 0, ql], g, QO0, right)
        arrived(vt.at[g, 1, qr], g, QR1)
        send(vt.at[g, 1, qr], vt.at[g, 1, qr], g, QO1, left)

    def opposite_across(g):
        for event, c, mate_event in ((O0, 0, QO0), (O1, 1, QO1)):
            arrived(vt.at[g, c, bo], g, event)
            send(vt.at[g, c, bo], vt.at[g, c, bo], g, mate_event, across)

    def finish_gather(g):
        for event, c, block in (
            (L1, 1, bl), (R0, 0, br), (O0, 0, bo), (O1, 1, bo), (QL0, 0, ql), (QR1, 1, qr),
            (QL1, 1, ql), (QR0, 0, qr), (QO0, 0, qo), (QO1, 1, qo),
        ):
            if event in ((QL0, QR1) if g < G - 1 else (O0, O1)):
                continue
            arrived(vt.at[g, c, block], g, event)

    c_copies = [
        pltpu.make_async_remote_copy(
            src_ref=coef.at[g, 1 - core], dst_ref=crecv.at[g], send_sem=c_send.at[g], recv_sem=c_recv.at[g],
            device_id=sibling, device_id_type=pl.DeviceIdType.MESH,
        )
        for g in range(G)
    ]
    def project(g):
        part = jnp.dot(vt[g, 0].reshape(128, -1), rhs1[...], preferred_element_type=jnp.float32)
        part = part + jnp.dot(vt[g, 1].reshape(128, -1), rhs2[...], preferred_element_type=jnp.float32)
        for half in range(2):
            for c in range(2):
                coef[g, half, c] = part[64 * half : 64 * half + 64, 128 * c : 128 * c + 128]
        c_copies[g].start()

    def far_first(j):
        return ZS // 2 + ((j + 1) // 2) * (2 * ((j + 1) % 2) - 1)

    def z_copy(g, k):
        return pltpu.make_async_remote_copy(
            src_ref=zsrc.at[g, (z + k) % ZS], dst_ref=zrecv.at[g, ZS - 1 - k],
            send_sem=z_send.at[g], recv_sem=z_recv.at[g],
            device_id=z_peer(k), device_id_type=pl.DeviceIdType.MESH,
        )

    def scatter_z(g):
        c_copies[g].wait_recv()
        zsrc[g] = (coef[g, core] + crecv[g]).reshape(ZS, 8, 128)

        for j in range(ZS - 1):
            z_copy(g, far_first(j)).start()

    def all_of(ref, send_sem, recv_sem):
        return pltpu.make_async_remote_copy(
            src_ref=ref, dst_ref=ref, send_sem=send_sem, recv_sem=recv_sem,
            device_id=right, device_id_type=pl.DeviceIdType.MESH,
        )

    def y_copy(g, k):
        return pltpu.make_async_remote_copy(
            src_ref=ysrc.at[g], dst_ref=yrecv.at[g, YL - 1 - k],
            send_sem=y_send.at[g], recv_sem=y_recv.at[g],
            device_id=y_peer(k), device_id_type=pl.DeviceIdType.MESH,
        )

    def exchange_y(g):
        all_of(zrecv.at[g], z_send.at[g], z_recv.at[g]).wait_recv()
        total = zsrc[g, z]
        for k in range(ZS - 1):
            total = total + zrecv[g, k]
        ysrc[g] = total
        for k in range(1, YL):
            y_copy(g, k).start()

    row = lax.broadcasted_iota(jnp.int32, (8, 128), 0)

    def s_copy(g, k):
        return pltpu.make_async_remote_copy(
            src_ref=sg.at[g, core, z], dst_ref=sg.at[g, core, z],
            send_sem=s_send.at[g], recv_sem=s_recv.at[g],
            device_id=at(x, y, k, core), device_id_type=pl.DeviceIdType.MESH,
        )

    def d_copy(g, k):
        return pltpu.make_async_remote_copy(
            src_ref=sg.at[g, core, z], dst_ref=sg.at[g, core, z],
            send_sem=d_send.at[g], recv_sem=d_recv.at[g],
            device_id=at(x, y, k, 1 - core), device_id_type=pl.DeviceIdType.MESH,
        )

    def scale(g):
        first = 64 * core + 8 * (z % 8)
        values = jnp.full((8, 128), lam[g, first], jnp.float32)
        for i in range(1, 8):
            values = jnp.where(row == i, lam[g, first + i], values)
        inverse = 1.0 / values
        all_of(yrecv.at[g], y_send.at[g], y_recv.at[g]).wait_recv()
        total = ysrc[g] + yrecv[g, 0] + yrecv[g, 1] + yrecv[g, 2]
        sg[g, core, z] = (total * inverse).astype(jnp.bfloat16)

        for target in range(ZS):
            if g in DIRECT:
                d_copy(g, target).start()

            @pl.when(z != target)
            def _(target=target):
                s_copy(g, target).start()

    def share(g):
        all_of(sg.at[g, core, pl.ds(0, ZS - 1)], s_send.at[g], s_recv.at[g]).wait_recv()
        if g not in DIRECT:
            pltpu.make_async_remote_copy(
                src_ref=sg.at[g, core], dst_ref=sg.at[g, core], send_sem=d_send.at[g], recv_sem=d_recv.at[g],
                device_id=sibling, device_id_type=pl.DeviceIdType.MESH,
            ).start()

    def transposed(g):
        for c in range(2):
            vrow[g, :, 128 * c : 128 * c + 128] = vt[g, c].reshape(128, -1).T

    def expand(g):
        all_of(sg.at[g, 1 - core], d_send.at[g], d_recv.at[g]).wait_recv()
        tiles = lambda part: [
            sg[g, half, part].astype(jnp.float32).reshape(64, 128) for half in range(2)
        ]
        re = jnp.concatenate(tiles(slice(0, 8)), axis=0).astype(jnp.bfloat16)
        im = jnp.concatenate(tiles(slice(8, 16)), axis=0).astype(jnp.bfloat16)
        factor = jnp.concatenate(
            [jnp.concatenate([re, im], axis=1), jnp.concatenate([-im, re], axis=1)], axis=0
        )
        product = jnp.dot(vrow[g], factor, preferred_element_type=jnp.float32)
        if g == 0:
            acc[...] = product
        elif g < G - 1:
            acc[...] += product
        else:
            total = (acc[...] + product).astype(out.dtype)
            out[0] = total[:, :128]
            out[1] = total[:, 128:]

    for g in range(G):
        start_own(g)
    for load in loads:
        load.wait()
    rhs2[:, 128:256] = -rhs1[:, 0:128]

    meet(0)
    relay_x(0)
    relay_x(1)
    meet(1)
    relay_x(2)
    start_mate(0)
    meet(2)
    opposite_across(2)
    start_mate(1)
    relay_mate(0)
    relay_mate(1)
    finish_gather(0)
    project(0)
    start_mate(2)
    meet(3)
    scatter_z(0)
    finish_gather(1)
    project(1)
    scatter_z(1)
    finish_gather(2)
    project(2)
    scatter_z(2)
    for g in range(G):
        transposed(g)
    exchange_y(0)
    exchange_y(1)
    scale(0)
    exchange_y(2)
    scale(1)
    scale(2)
    share(0)
    expand(0)
    share(1)
    expand(1)
    share(2)
    expand(2)

    for copy in sent:
        copy.wait_send()
    for g in range(G):
        c_copies[g].wait_send()
        all_of(sg.at[g, core], d_send.at[g], d_recv.at[g]).wait_send()
        all_of(zrecv.at[g], z_send.at[g], z_recv.at[g]).wait_send()
        all_of(yrecv.at[g], y_send.at[g], y_recv.at[g]).wait_send()
        all_of(sg.at[g, core, pl.ds(0, ZS - 1)], s_send.at[g], s_recv.at[g]).wait_send()


def on_device(vectors, lambdas, sources):
    rows = sources.shape[1]
    cols = sources.shape[2]
    vec = jnp.transpose(vectors, (0, 1, 3, 2))
    f32, bf16 = jnp.float32, jnp.bfloat16
    dma = pltpu.SemaphoreType.DMA
    total = pl.pallas_call(
        kernel,
        out_shape=pltpu.VMEM((2, rows, cols), bf16),
        in_specs=[
            pl.BlockSpec(memory_space=pl.ANY),
            pl.BlockSpec(memory_space=pltpu.SMEM),
            pl.BlockSpec(memory_space=pl.ANY),
        ],
        out_specs=pl.BlockSpec(memory_space=pltpu.VMEM),
        scratch_shapes=[
            pltpu.VMEM((G, 2, 8, 16, rows), bf16),
            pltpu.VMEM((G, rows, 256), bf16),
            pltpu.VMEM((rows, 256), bf16),
            pltpu.VMEM((rows, 256), bf16),
            pltpu.VMEM((rows, 256), f32),
            pltpu.VMEM((G, 2, 2, 64, 128), f32),
            pltpu.VMEM((G, 2, 64, 128), f32),
            pltpu.VMEM((G, ZS, 8, 128), f32),
            pltpu.VMEM((G, ZS - 1, 8, 128), f32),
            pltpu.VMEM((G, 8, 128), f32),
            pltpu.VMEM((G, YL - 1, 8, 128), f32),
            pltpu.VMEM((G, 2, ZS, 8, 128), bf16),
            pltpu.SemaphoreType.REGULAR((4,)),
            dma((4,)),
            dma((G, EVENTS)),
            dma((G, EVENTS)),
            dma((G,)), dma((G,)), dma((G,)), dma((G,)), dma((G,)), dma((G,)),
            dma((G,)), dma((G,)), dma((G,)), dma((G,)),
        ],
        compiler_params=pltpu.CompilerParams(collective_id=0, has_side_effects=True),
    )(vec, lambdas, sources)
    return total


def solution(mesh):
    placed = (P(None, None, "space", "src"), P(), P(None, "space", "src"))
    return jax.shard_map(
        on_device, mesh=mesh, in_specs=placed, out_specs=P(None, "space", "src"), check_vma=False
    )
```
